128 devices in a mesh: dom: 128 (over y, x, z, core).
Axes of the slice: x: 4, y: 4, z: 4, core: 2. Of those that a mesh axis runs over, the one named last changes fastest.
Arguments:
- matrix_tiles: bfloat16 [3072, 27, 128, 128], P('dom'), may hold values from -20 to 20, as said below
- tentative: bfloat16 [3072, 6, 128], P('dom'), may hold values from -0.59765625 to 0.59765625
- column_slots: int32 [3072, 27], P('dom'), may hold values from 0 to 87, as said below
- send_list: int32 [128, 4, 16], P('dom'), may hold values from 0 to 23
- column_aggregate: int32 [3072, 27], P('dom'), may hold values from 0 to 1023, as said below
Outputs:
- coarse: float32 [1024, 6, 432], P('dom')
The draws below stay inside these ranges and needn't reach their ends.
Inputs may be any that keep to these rules, and one draw needn't show every extreme that they name: column_slots[b, 0] is b's own index in its partition; slots below 24 name own blocks, the last 9 slots of a row name received blocks, only from partitions that exist. column_aggregate names the aggregate of the block that the slot refers to; each aggregate is three blocks of one partition, and the aggregates of partition d are d * 8 to d * 8 + 7. matrix_tiles[b, 0, i, i] lies between 2 and 20.
All inputs are finite; a program needn't handle non-finite values.
Results may differ from the reference program's by a relative error of at most 0.0003.
Values may be sent and summed in bfloat16 or wider, within the bound.
A program may use at most 64 MiB of HBM per device.

```python
import math
import jax
import jax.numpy as jnp
from jax import lax

BS = 128
MODES = 6
K = 27
KG = 9
R = 2
GH = 16
RB = 24
NBLK = 3072
AGG_DEV = 8
NAGG = 1024
N_DOM = 128


def block_layout(key):
    device = jnp.arange(N_DOM, dtype=jnp.int32)
    send_table = jax.random.randint(jax.random.fold_in(key, 101), (N_DOM, 2 * R, GH), 0, RB, dtype=jnp.int32)
    order_keys = jax.random.split(jax.random.fold_in(key, 102), N_DOM)
    ordering = jax.vmap(lambda one_key: jax.random.permutation(one_key, RB))(order_keys).astype(jnp.int32)
    local_slots = jax.random.randint(jax.random.fold_in(key, 103), (N_DOM, RB, K - KG - 1), 0, RB, dtype=jnp.int32)
    peer_slot = jax.random.randint(jax.random.fold_in(key, 104), (N_DOM, RB, KG), 0, 2 * R, dtype=jnp.int32)
    within = jax.random.randint(jax.random.fold_in(key, 105), (N_DOM, RB, KG), 0, GH, dtype=jnp.int32)
    peer_slot = peer_slot.at[N_DOM - 1, RB - 1, KG - 1].set(2 * R - 1)
    within = within.at[N_DOM - 1, RB - 1, KG - 1].set(GH - 1)
    offset = jnp.where(peer_slot < R, peer_slot - R, peer_slot - R + 1)
    source = device[:, None, None] - offset
    invalid = (source < 0) | (source >= N_DOM)
    peer_slot = jnp.where(invalid, 2 * R - 1 - peer_slot, peer_slot)
    offset = jnp.where(peer_slot < R, peer_slot - R, peer_slot - R + 1)
    source = device[:, None, None] - offset
    self_slot = jnp.broadcast_to(jnp.arange(RB, dtype=jnp.int32)[None, :, None], (N_DOM, RB, 1))
    slots = jnp.concatenate([self_slot, local_slots, RB + peer_slot * GH + within], axis=2)
    local_agg = device[:, None] * AGG_DEV + ordering // 3
    self_agg = local_agg[:, :, None]
    near_agg = jnp.take_along_axis(local_agg, local_slots.reshape(N_DOM, -1), axis=1).reshape(local_slots.shape)
    ghost_block = send_table[source, peer_slot, within]
    ghost_agg = local_agg[source, ghost_block]
    aggregates = jnp.concatenate([self_agg, near_agg, ghost_agg], axis=2)
    return (slots.reshape(NBLK, K).astype(jnp.int32), send_table, aggregates.reshape(NBLK, K).astype(jnp.int32))


def draw_column_slots(key, part):
    return block_layout(key)[0]


def draw_send_list(key, part):
    return block_layout(key)[1]


def draw_column_aggregate(key, part):
    return block_layout(key)[2]


def draw_matrix_tiles(key, part):
    shape = (NBLK, K, BS, BS)
    noise_key = jax.random.fold_in(key, 201)
    lead_key = jax.random.fold_in(key, 202)
    noise = jax.random.normal(noise_key, shape, jnp.float32)
    leading = jnp.exp(jax.random.uniform(lead_key, (NBLK, BS), jnp.float32, math.log(2.0), math.log(20.0)))
    noise = noise * (BS * K) ** (-0.5)
    identity = jnp.eye(BS, dtype=jnp.float32) > 0.5
    first_slot = (jnp.arange(K) == 0)[None, :, None, None]
    tiles = jnp.where(first_slot & identity[None, None], leading[:, None, :, None], noise)
    return tiles.astype(jnp.bfloat16)


def steps_of(stream_key, dims, cuts, low, high):
    gain, own = 1.0, jax.random.fold_in(stream_key, 6)
    for axis_at, parts in cuts:
        heights = jnp.exp(jax.random.uniform(jax.random.fold_in(own, axis_at), (parts,), jnp.float32, low / len(cuts), high / len(cuts)))
        gain = gain * jnp.repeat(heights, dims[axis_at] // parts).reshape([-1 if axis == axis_at else 1 for axis in range(len(dims))])
    return gain


def bell_draw(stream_key, extent, deviation, limit, shards=(), kind=jnp.bfloat16):
    entries = deviation * jax.random.normal(stream_key, extent, jnp.float32)
    if shards:
        entries = entries * steps_of(stream_key, extent, shards, -0.22, 0.18)
    return jnp.clip(entries, -limit, limit).astype(kind)


def setup_inputs(seed: int = 0) -> dict:
    splits = jax.random.split(jax.random.key(seed), 6)
    return {
        "matrix_tiles": draw_matrix_tiles(jax.random.fold_in(splits[5], 71), 0),
        "tentative": bell_draw(splits[1], (NBLK, MODES, BS), 0.1, 0.59765625, ((0, 128),)),
        "column_slots": draw_column_slots(jax.random.fold_in(splits[5], 71), 0),
        "send_list": draw_send_list(jax.random.fold_in(splits[5], 71), 0),
        "column_aggregate": draw_column_aggregate(jax.random.fold_in(splits[5], 71), 0),
    }


OMEGA = 0.6


def slot_blocks(column_slots, send_list):
    device = jnp.arange(NBLK, dtype=jnp.int32) // RB
    is_local = column_slots < RB
    ghost_slot = jnp.maximum(column_slots - RB, 0)
    peer_slot = ghost_slot // GH
    within = ghost_slot % GH
    offset = jnp.where(peer_slot < R, peer_slot - R, peer_slot - R + 1)
    source = jnp.clip(device[:, None] - offset, 0, N_DOM - 1)
    remote = source * RB + send_list[source, peer_slot, within]
    return jnp.where(is_local, device[:, None] * RB + column_slots, remote).astype(jnp.int32)


def place_blocks(partial_value, row_agg, col_agg, values, row_base, agg_count):
    row_index = (row_agg - row_base).astype(jnp.int32)
    col_index = (col_agg - (row_agg // agg_count - 2 * R) * agg_count).astype(jnp.int32)
    return partial_value.at[row_index, :, col_index, :].add(values)


def reference(matrix_tiles, tentative, column_slots, send_list, column_aggregate):
    block_ids = slot_blocks(column_slots, send_list)
    window = (4 * R + 1) * AGG_DEV

    def section(coarse, device):
        first_row = (device * RB).astype(jnp.int32)
        block_tiles = lax.dynamic_slice_in_dim(matrix_tiles, first_row, RB, 0).astype(jnp.float32)
        own_modes = lax.dynamic_slice_in_dim(tentative, first_row, RB, 0).astype(jnp.float32)
        row_ids = lax.dynamic_slice_in_dim(block_ids, first_row, RB, 0)
        aggregates = lax.dynamic_slice_in_dim(column_aggregate, first_row, RB, 0)
        columns = tentative[row_ids].astype(jnp.float32)
        product = jnp.einsum('bsij,bsmj->bsmi', block_tiles, columns, precision=lax.Precision.HIGHEST)
        inverse = 1.0 / jnp.diagonal(block_tiles[:, 0], axis1=1, axis2=2)
        direct_term = jnp.einsum('bmi,bsni->bsmn', own_modes, product, precision=lax.Precision.HIGHEST)
        smooth_term = -OMEGA * jnp.einsum('bsmi,bi,btni->bstmn', product, inverse, product, precision=lax.Precision.HIGHEST)
        row_first = jnp.broadcast_to(aggregates[:, :1], aggregates.shape)
        coarse = place_blocks(coarse, row_first, aggregates, direct_term, 0, AGG_DEV)
        pair_rows = jnp.broadcast_to(aggregates[:, :, None], (RB, K, K))
        pair_cols = jnp.broadcast_to(aggregates[:, None, :], (RB, K, K))
        coarse = place_blocks(coarse, pair_rows, pair_cols, smooth_term, 0, AGG_DEV)
        return coarse, None

    start = jnp.zeros((NAGG, MODES, window, MODES), jnp.float32)
    coarse, unused = lax.scan(section, start, jnp.arange(N_DOM, dtype=jnp.int32))
    return coarse.reshape(NAGG, MODES, window * MODES)
```

```python
import functools

import jax
import jax.numpy as jnp
from jax import lax
from jax.experimental import pallas as pl
from jax.experimental.pallas import tpu as pltpu
from jax.sharding import PartitionSpec as P

OMEGA = 0.6
RB = 24
K = 27
KO = 18
KG = 9
BS = 128
MODES = 6
GH = 16
SLAB = 48
SPAN = 5 * SLAB
OFFSETS = (-2, -1, 1, 2)
NT = (((1,), (1,)), ((), ()))
U_OWN = 4
U_GH = 4
MESH = pl.DeviceIdType.MESH

dot = functools.partial(lax.dot_general, dimension_numbers=NT, preferred_element_type=jnp.float32)


def expand(x, row_agg):
    r2, r4, r6 = (pltpu.roll(x, s, 0) for s in (2, 4, 6))
    i = lax.broadcasted_iota(jnp.int32, (8, BS), 0)
    v = (jnp.where(i < 6, x, r6), jnp.where(i < 4, r6, r4), jnp.where(i < 2, r4, r2))
    agg = jnp.broadcast_to(x[6:7, :], (8, BS))
    rows = [jnp.where(row_agg[8 * k : 8 * k + 8] == agg, v[k % 3], 0.0) for k in range(6)]
    return jnp.concatenate(rows, axis=0).astype(jnp.bfloat16)


def split(x):
    high = x.astype(jnp.bfloat16)
    low = (x - high.astype(jnp.float32)).astype(jnp.bfloat16)
    return high, low


def kernel(
    count,
    a_hbm, t_hbm, slots_hbm, send_hbm, agg_hbm,
    out_ref,
    a_v, t_v, t8, te_own, te_gh, send_t, recv_t, g_own, weight, acc, send_c, recv_c, result,
    slots, send_list, agg,
    a_sem, small_sem, st_sem, rt_sem, sc_sem, rc_sem,
):
    me = lax.axis_index("dom")
    small = [
        pltpu.make_async_copy(src, dst, small_sem.at[i])
        for i, (src, dst) in enumerate(
            ((agg_hbm, agg), (t_hbm, t_v), (send_hbm, send_list), (slots_hbm, slots))
        )
    ]
    for copy in small:
        copy.start()

    def own_copy(b):
        return pltpu.make_async_copy(
            a_hbm.at[b, pl.ds(0, KO)], a_v.at[b, pl.ds(0, KO)], a_sem.at[0, b]
        )

    def ghost_copy(b):
        return pltpu.make_async_copy(
            a_hbm.at[b, pl.ds(KO, KG)], a_v.at[b, pl.ds(KO, KG)], a_sem.at[1, b]
        )

    for b in range(RB):
        own_copy(b).start()
    for b in range(RB):
        ghost_copy(b).start()

    exists = [jnp.logical_and(me - o >= 0, me - o < count) for o in OFFSETS]
    recv_c[...] = jnp.zeros_like(recv_c)
    barrier = pltpu.get_barrier_semaphore()
    for p, o in enumerate(OFFSETS):
        @pl.when(exists[p])
        def _():
            pl.semaphore_signal(barrier, inc=1, device_id=(me - o,), device_id_type=MESH)

    iota = lax.broadcasted_iota(jnp.int32, (SLAB, BS), 0)
    row_agg = lax.shift_right_logical(iota * 43, 8).astype(jnp.float32)

    small[0].wait()
    small[1].wait()
    for m in range(MODES):
        t8[:, m, :] = t_v[m].astype(jnp.float32)
    for b in range(RB):
        own_agg = (agg[b, 0] - me * 8).astype(jnp.float32)
        t8[b, MODES:8, :] = jnp.full((2, BS), own_agg, jnp.float32)
    small[2].wait()
    for p in range(4):
        for g in range(0, GH, 2):
            pair = [t8[send_list[0, p, g + h]] for h in range(2)]
            send_t[p, g * 8 : g * 8 + 16, :] = jnp.concatenate(pair, axis=0).astype(jnp.bfloat16)

    def own_table(b, c):
        te_own[b] = expand(t8[b], row_agg)
        return c

    lax.fori_loop(0, RB, own_table, 0, unroll=4)

    total = sum(e.astype(jnp.int32) for e in exists)
    pl.semaphore_wait(barrier, total)

    def t_copy(p):
        return pltpu.make_async_remote_copy(
            src_ref=send_t.at[p], dst_ref=recv_t.at[p], send_sem=st_sem.at[p], recv_sem=rt_sem.at[p],
            device_id=(me + OFFSETS[p],), device_id_type=MESH,
        )

    for p in range(4):
        @pl.when(exists[3 - p])
        def _():
            t_copy(p).start()

    def zero_table(v, c):
        te_gh[v] = jnp.zeros((4 * SLAB, BS), jnp.bfloat16)
        return c

    lax.fori_loop(0, 4 * GH, zero_table, 0, unroll=4)
    small[3].wait()

    eye = lax.broadcasted_iota(jnp.int32, (BS, BS), 0) == lax.broadcasted_iota(jnp.int32, (BS, BS), 1)

    def own_rows(step, c):
        for u in range(U_OWN):
            b = step * U_OWN + u
            own_copy(b).wait()
            lhs = jnp.concatenate([te_own[slots[b, s]] for s in range(KO)], axis=1)
            rhs = jnp.concatenate([a_v[b, s] for s in range(KO)], axis=1)
            g_own[b] = dot(lhs, rhs)
            diagonal = jnp.sum(
                jnp.where(eye, a_v[b, 0].astype(jnp.float32), 0.0), axis=0, keepdims=True
            )
            weight[b] = jnp.broadcast_to(-OMEGA * (1.0 / diagonal), (8, BS))
        return c

    lax.fori_loop(0, RB // U_OWN, own_rows, 0)

    for p in range(4):
        @pl.when(exists[p])
        def _():
            t_copy(p).wait_recv()

    for p in range(4):
        def ghost_table(g, c):
            x = recv_t[p, pl.ds(pl.multiple_of(g * 16, 16), 16), :].astype(jnp.float32)
            rows = slice((3 - p) * SLAB, (4 - p) * SLAB)
            te_gh[p * GH + 2 * g, rows, :] = expand(x[0:8], row_agg)
            te_gh[p * GH + 2 * g + 1, rows, :] = expand(x[8:16], row_agg)
            return c

        lax.fori_loop(0, GH // 2, ghost_table, 0, unroll=2)

    acc[...] = jnp.zeros_like(acc)

    def ghost_rows(step, c):
        lefts, rights = ([], []), ([], [])
        for u in range(U_GH):
            b = step * U_GH + u
            ghost_copy(b).wait()
            lhs = jnp.concatenate([te_gh[jnp.maximum(slots[b, s] - RB, 0)] for s in range(KO, K)], axis=1)
            rhs = jnp.concatenate([a_v[b, s] for s in range(KO, K)], axis=1)
            ghost = dot(lhs, rhs)
            own = g_own[b]
            w = weight[b, 0:1]
            own_left = te_own[b].astype(jnp.float32) + own * w
            grouped = jnp.concatenate([ghost[: 2 * SLAB], own, ghost[2 * SLAB :]], axis=0)
            left = jnp.concatenate([ghost[: 2 * SLAB] * w, own_left, ghost[2 * SLAB :] * w], axis=0)
            for whole, parts in ((grouped, rights), (left, lefts)):
                high, low = split(whole)
                parts[0].append(high)
                parts[1].append(low)
        lhs = jnp.concatenate(lefts[0] + lefts[0] + lefts[1], axis=1)
        rhs = jnp.concatenate(rights[0] + rights[1] + rights[0], axis=1)
        acc[...] += dot(lhs, rhs)
        return c

    lax.fori_loop(0, RB // U_GH, ghost_rows, 0)

    def c_copy(p):
        return pltpu.make_async_remote_copy(
            src_ref=send_c.at[p], dst_ref=recv_c.at[p], send_sem=sc_sem.at[p], recv_sem=rc_sem.at[p],
            device_id=(me - OFFSETS[p],), device_id_type=MESH,
        )

    for p, o in enumerate(OFFSETS):
        slab = 2 - o
        send_c[p, :, 0:SPAN] = acc[slab * SLAB : (slab + 1) * SLAB, :].astype(jnp.bfloat16)
        send_c[p, :, SPAN:256] = jnp.zeros((SLAB, 256 - SPAN), jnp.bfloat16)
    for p in range(4):
        @pl.when(exists[p])
        def _():
            c_copy(p).start()

    lane = lax.broadcasted_iota(jnp.int32, (SLAB, 256), 1)
    zeros = jnp.zeros((SLAB, 256), jnp.float32)

    def placed(x, by):
        wide = jnp.concatenate([x, zeros], axis=1)
        return wide if by == 0 else pltpu.roll(wide, by, 1)

    g_own[0, :, :] = acc[2 * SLAB : 3 * SLAB, 0:128]
    g_own[1, :, :] = jnp.zeros((SLAB, BS), jnp.float32)
    g_own[1, :, 0 : SPAN - 128] = acc[2 * SLAB : 3 * SLAB, 128:SPAN]
    summed = placed(jnp.concatenate([g_own[0], g_own[1]], axis=1), 2 * SLAB)
    for p, o in enumerate(OFFSETS):
        @pl.when(exists[3 - p])
        def _():
            c_copy(p).wait_recv()
    for p, o in enumerate(OFFSETS):
        summed = summed + placed(recv_c[p].astype(jnp.float32), (o + 2) * SLAB)
    for t in range(4):
        result[t] = summed[:, t * BS : (t + 1) * BS]
    for m in range(MODES):
        for t in range(4):
            size = min(BS, 9 * SLAB - t * BS)
            rows = result[t, pl.ds(m, 8, stride=MODES), :]
            out_ref[m, :, t * BS : t * BS + size] = rows[:, :size]
    for p in range(4):
        @pl.when(exists[3 - p])
        def _():
            t_copy(p).wait_send()

        @pl.when(exists[p])
        def _():
            c_copy(p).wait_send()


def solution(mesh):
    count = mesh.shape["dom"]
    call = pl.pallas_call(
        functools.partial(kernel, count),
        out_shape=jax.ShapeDtypeStruct((MODES, 8, 9 * SLAB), jnp.float32),
        in_specs=[pl.BlockSpec(memory_space=pl.ANY)] * 5,
        out_specs=pl.BlockSpec(memory_space=pltpu.VMEM),
        scratch_shapes=[
            pltpu.VMEM((RB, K, BS, BS), jnp.bfloat16),
            pltpu.VMEM((MODES, RB, BS), jnp.bfloat16),
            pltpu.VMEM((RB, 8, BS), jnp.float32),
            pltpu.VMEM((RB, SLAB, BS), jnp.bfloat16),
            pltpu.VMEM((4 * GH, 4 * SLAB, BS), jnp.bfloat16),
            pltpu.VMEM((4, GH * 8, BS), jnp.bfloat16),
            pltpu.VMEM((4, GH * 8, BS), jnp.bfloat16),
            pltpu.VMEM((RB, SLAB, BS), jnp.float32),
            pltpu.VMEM((RB, 8, BS), jnp.float32),
            pltpu.VMEM((SPAN, SPAN), jnp.float32),
            pltpu.VMEM((4, SLAB, 256), jnp.bfloat16),
            pltpu.VMEM((4, SLAB, 256), jnp.bfloat16),
            pltpu.VMEM((4, SLAB, BS), jnp.float32),
            pltpu.SMEM((RB, K), jnp.int32),
            pltpu.SMEM((1, 4, GH), jnp.int32),
            pltpu.SMEM((RB, K), jnp.int32),
            pltpu.SemaphoreType.DMA((2, RB)),
            pltpu.SemaphoreType.DMA((4,)),
            pltpu.SemaphoreType.DMA((4,)),
            pltpu.SemaphoreType.DMA((4,)),
            pltpu.SemaphoreType.DMA((4,)),
            pltpu.SemaphoreType.DMA((4,)),
        ],
        compiler_params=pltpu.CompilerParams(
            collective_id=0, has_side_effects=True, vmem_limit_bytes=56 << 20
        ),
    )

    def body(matrix_tiles, tentative, column_slots, send_list, column_aggregate):
        by_mode = call(
            matrix_tiles, tentative.transpose(1, 0, 2), column_slots, send_list, column_aggregate
        )
        return by_mode.transpose(1, 0, 2)

    placed = (
        P("dom", None, None, None),
        P("dom", None, None),
        P("dom", None),
        P("dom", None, None),
        P("dom", None),
    )
    return jax.shard_map(
        body, mesh=mesh, in_specs=placed, out_specs=P("dom", None, None), check_vma=False
    )
```

```python
import functools

import jax
import jax.numpy as jnp
from jax import lax
from jax.experimental import pallas as pl
from jax.experimental.pallas import tpu as pltpu
from jax.sharding import PartitionSpec as P

OMEGA = 0.6
RB = 24
K = 27
KO = 18
KG = 9
BS = 128
MODES = 6
GH = 16
SLAB = 48
SPAN = 5 * SLAB
OFFSETS = (-2, -1, 1, 2)
NT = (((1,), (1,)), ((), ()))
U_OWN = 4
U_GH = 8
STREAMED = 8
MESH = pl.DeviceIdType.MESH

dot = functools.partial(lax.dot_general, dimension_numbers=NT, preferred_element_type=jnp.float32)


def expand(x, row_agg):
    r2, r4, r6 = (pltpu.roll(x, s, 0) for s in (2, 4, 6))
    i = lax.broadcasted_iota(jnp.int32, (8, BS), 0)
    v = (jnp.where(i < 6, x, r6), jnp.where(i < 4, r6, r4), jnp.where(i < 2, r4, r2))
    agg = jnp.broadcast_to(x[6:7, :], (8, BS))
    rows = [jnp.where(row_agg[8 * k : 8 * k + 8] == agg, v[k % 3], 0.0) for k in range(6)]
    return jnp.concatenate(rows, axis=0).astype(jnp.bfloat16)


def split(x):
    high = x.astype(jnp.bfloat16)
    low = (x - high.astype(jnp.float32)).astype(jnp.bfloat16)
    return high, low


def kernel(
    count,
    a_hbm, t_hbm, slots_hbm, send_hbm, agg_hbm,
    out_ref,
    a_v, t_v, t8, te_own, te_gh, send_t, recv_t, g_own, weight, acc, send_c, recv_c, result,
    slots, send_list, agg,
    a_sem, small_sem, st_sem, rt_sem, sc_sem, rc_sem,
):
    me = lax.axis_index("dom")
    small = [
        pltpu.make_async_copy(src, dst, small_sem.at[i])
        for i, (src, dst) in enumerate(
            ((agg_hbm, agg), (t_hbm, t_v), (send_hbm, send_list), (slots_hbm, slots))
        )
    ]
    for copy in small:
        copy.start()

    def own_copy(step):
        part = (pl.ds(step * U_OWN, U_OWN), pl.ds(0, KO))
        return pltpu.make_async_copy(a_hbm.at[part], a_v.at[part], a_sem.at[0, step])

    def ghost_copy(step):
        part = (pl.ds(step * U_GH, U_GH), pl.ds(KO, KG))
        return pltpu.make_async_copy(a_hbm.at[part], a_v.at[part], a_sem.at[1, step])


    exists = [jnp.logical_and(me - o >= 0, me - o < count) for o in OFFSETS]
    recv_c[...] = jnp.zeros_like(recv_c)
    barrier = pltpu.get_barrier_semaphore()
    for p, o in enumerate(OFFSETS):
        @pl.when(exists[p])
        def _():
            pl.semaphore_signal(barrier, inc=1, device_id=(me - o,), device_id_type=MESH)

    own_copy(0).start()
    for copy in small:
        copy.wait()
    for step in range(1, RB // U_OWN):
        own_copy(step).start()
    for step in range(RB // U_GH):
        ghost_copy(step).start()

    iota = lax.broadcasted_iota(jnp.int32, (SLAB, BS), 0)
    row_agg = lax.shift_right_logical(iota * 43, 8).astype(jnp.float32)

    for m in range(MODES):
        t8[:, m, :] = t_v[m].astype(jnp.float32)
    for b in range(RB):
        own_agg = (agg[b, 0] - me * 8).astype(jnp.float32)
        t8[b, MODES:8, :] = jnp.full((2, BS), own_agg, jnp.float32)
    for p in range(4):
        for g in range(0, GH, 2):
            pair = [t8[send_list[0, p, g + h]] for h in range(2)]
            send_t[p, g * 8 : g * 8 + 16, :] = jnp.concatenate(pair, axis=0).astype(jnp.bfloat16)

    def own_table(b, c):
        te_own[b] = expand(t8[b], row_agg)
        return c

    lax.fori_loop(0, RB, own_table, 0, unroll=4)

    total = sum(e.astype(jnp.int32) for e in exists)
    pl.semaphore_wait(barrier, total)

    def t_copy(p):
        return pltpu.make_async_remote_copy(
            src_ref=send_t.at[p], dst_ref=recv_t.at[p], send_sem=st_sem.at[p], recv_sem=rt_sem.at[p],
            device_id=(me + OFFSETS[p],), device_id_type=MESH,
        )

    for p in range(4):
        @pl.when(exists[3 - p])
        def _():
            t_copy(p).start()

    def zero_table(v, c):
        te_gh[v] = jnp.zeros((4 * SLAB, BS), jnp.bfloat16)
        return c

    lax.fori_loop(0, 4 * GH, zero_table, 0, unroll=4)

    eye = lax.broadcasted_iota(jnp.int32, (BS, BS), 0) == lax.broadcasted_iota(jnp.int32, (BS, BS), 1)

    def own_rows(step, c):
        own_copy(step).wait()
        for u in range(U_OWN):
            b = step * U_OWN + u
            still, moving = range(KO - STREAMED), range(KO - STREAMED, KO)
            table, tiles = (
                [jnp.concatenate([f(s) for s in part], axis=1) for part in (still, moving)]
                for f in (lambda s: te_own[slots[b, s]], lambda s: a_v[b, s])
            )
            g_own[b] = dot(table[0], tiles[0]) + dot(tiles[1], table[1]).T
            diagonal = jnp.sum(
                jnp.where(eye, a_v[b, 0].astype(jnp.float32), 0.0), axis=0, keepdims=True
            )
            weight[b] = jnp.broadcast_to(-OMEGA * (1.0 / diagonal), (8, BS))
        return c

    lax.fori_loop(0, RB // U_OWN, own_rows, 0)

    for p in range(4):
        @pl.when(exists[p])
        def _():
            t_copy(p).wait_recv()

    for p in range(4):
        def ghost_table(g, c):
            x = recv_t[p, pl.ds(pl.multiple_of(g * 16, 16), 16), :].astype(jnp.float32)
            rows = slice((3 - p) * SLAB, (4 - p) * SLAB)
            te_gh[p * GH + 2 * g, rows, :] = expand(x[0:8], row_agg)
            te_gh[p * GH + 2 * g + 1, rows, :] = expand(x[8:16], row_agg)
            return c

        lax.fori_loop(0, GH // 2, ghost_table, 0, unroll=2)

    acc[...] = jnp.zeros_like(acc)

    def ghost_rows(step, c):
        lefts, rights = ([], []), ([], [])
        ghost_copy(step).wait()
        for u in range(U_GH):
            b = step * U_GH + u
            lhs = jnp.concatenate([te_gh[jnp.maximum(slots[b, s] - RB, 0)] for s in range(KO, K)], axis=1)
            rhs = jnp.concatenate([a_v[b, s] for s in range(KO, K)], axis=1)
            ghost = dot(lhs, rhs)
            own = g_own[b]
            w = weight[b, 0:1]
            own_left = te_own[b].astype(jnp.float32) + own * w
            grouped = jnp.concatenate([ghost[: 2 * SLAB], own, ghost[2 * SLAB :]], axis=0)
            left = jnp.concatenate([ghost[: 2 * SLAB] * w, own_left, ghost[2 * SLAB :] * w], axis=0)
            for whole, parts in ((grouped, rights), (left, lefts)):
                high, low = split(whole)
                parts[0].append(high)
                parts[1].append(low)
        lhs = jnp.concatenate(lefts[0] + lefts[0] + lefts[1], axis=1)
        rhs = jnp.concatenate(rights[0] + rights[1] + rights[0], axis=1)
        acc[...] += dot(lhs, rhs)
        return c

    lax.fori_loop(0, RB // U_GH, ghost_rows, 0)

    def c_copy(p):
        return pltpu.make_async_remote_copy(
            src_ref=send_c.at[p], dst_ref=recv_c.at[p], send_sem=sc_sem.at[p], recv_sem=rc_sem.at[p],
            device_id=(me - OFFSETS[p],), device_id_type=MESH,
        )

    for p, o in enumerate(OFFSETS):
        slab = 2 - o
        send_c[p, :, 0:SPAN] = acc[slab * SLAB : (slab + 1) * SLAB, :].astype(jnp.bfloat16)
        send_c[p, :, SPAN:256] = jnp.zeros((SLAB, 256 - SPAN), jnp.bfloat16)
    for p in range(4):
        @pl.when(exists[p])
        def _():
            c_copy(p).start()

    lane = lax.broadcasted_iota(jnp.int32, (SLAB, 256), 1)
    zeros = jnp.zeros((SLAB, 256), jnp.float32)

    def placed(x, by):
        wide = jnp.concatenate([x, zeros], axis=1)
        return wide if by == 0 else pltpu.roll(wide, by, 1)

    g_own[0, :, :] = acc[2 * SLAB : 3 * SLAB, 0:128]
    g_own[1, :, :] = jnp.zeros((SLAB, BS), jnp.float32)
    g_own[1, :, 0 : SPAN - 128] = acc[2 * SLAB : 3 * SLAB, 128:SPAN]
    summed = placed(jnp.concatenate([g_own[0], g_own[1]], axis=1), 2 * SLAB)
    for p, o in enumerate(OFFSETS):
        @pl.when(exists[3 - p])
        def _():
            c_copy(p).wait_recv()
    for p, o in enumerate(OFFSETS):
        summed = summed + placed(recv_c[p].astype(jnp.float32), (o + 2) * SLAB)
    for t in range(4):
        result[t] = summed[:, t * BS : (t + 1) * BS]
    for m in range(MODES):
        for t in range(4):
            size = min(BS, 9 * SLAB - t * BS)
            rows = result[t, pl.ds(m, 8, stride=MODES), :]
            out_ref[m, :, t * BS : t * BS + size] = rows[:, :size]
    for p in range(4):
        @pl.when(exists[3 - p])
        def _():
            t_copy(p).wait_send()

        @pl.when(exists[p])
        def _():
            c_copy(p).wait_send()


def solution(mesh):
    count = mesh.shape["dom"]
    call = pl.pallas_call(
        functools.partial(kernel, count),
        out_shape=pltpu.VMEM((MODES, 8, 9 * SLAB), jnp.float32),
        in_specs=[pl.BlockSpec(memory_space=pl.ANY)] * 5,
        out_specs=pl.BlockSpec(memory_space=pltpu.VMEM),
        scratch_shapes=[
            pltpu.VMEM((RB, K, BS, BS), jnp.bfloat16),
            pltpu.VMEM((MODES, RB, BS), jnp.bfloat16),
            pltpu.VMEM((RB, 8, BS), jnp.float32),
            pltpu.VMEM((RB, SLAB, BS), jnp.bfloat16),
            pltpu.VMEM((4 * GH, 4 * SLAB, BS), jnp.bfloat16),
            pltpu.VMEM((4, GH * 8, BS), jnp.bfloat16),
            pltpu.VMEM((4, GH * 8, BS), jnp.bfloat16),
            pltpu.VMEM((RB, SLAB, BS), jnp.float32),
            pltpu.VMEM((RB, 8, BS), jnp.float32),
            pltpu.VMEM((SPAN, SPAN), jnp.float32),
            pltpu.VMEM((4, SLAB, 256), jnp.bfloat16),
            pltpu.VMEM((4, SLAB, 256), jnp.bfloat16),
            pltpu.VMEM((4, SLAB, BS), jnp.float32),
            pltpu.SMEM((RB, K), jnp.int32),
            pltpu.SMEM((1, 4, GH), jnp.int32),
            pltpu.SMEM((RB, K), jnp.int32),
            pltpu.SemaphoreType.DMA((2, RB)),
            pltpu.SemaphoreType.DMA((4,)),
            pltpu.SemaphoreType.DMA((4,)),
            pltpu.SemaphoreType.DMA((4,)),
            pltpu.SemaphoreType.DMA((4,)),
            pltpu.SemaphoreType.DMA((4,)),
        ],
        compiler_params=pltpu.CompilerParams(
            collective_id=0, has_side_effects=True, vmem_limit_bytes=56 << 20
        ),
    )

    def body(matrix_tiles, tentative, column_slots, send_list, column_aggregate):
        by_mode = call(
            matrix_tiles, tentative.transpose(1, 0, 2), column_slots, send_list, column_aggregate
        )
        return by_mode.transpose(1, 0, 2)

    placed = (
        P("dom", None, None, None),
        P("dom", None, None),
        P("dom", None),
        P("dom", None, None),
        P("dom", None),
    )
    return jax.shard_map(
        body, mesh=mesh, in_specs=placed, out_specs=P("dom", None, None), check_vma=False
    )
```

```python
import functools

import jax
import jax.numpy as jnp
from jax import lax
from jax.experimental import pallas as pl
from jax.experimental.pallas import tpu as pltpu
from jax.sharding import PartitionSpec as P

OMEGA = 0.6
RB = 24
K = 27
KO = 18
KG = 9
BS = 128
MODES = 6
GH = 16
SLAB = 48
SPAN = 5 * SLAB
OFFSETS = (-2, -1, 1, 2)
NT = (((1,), (1,)), ((), ()))
OWN = slice(2 * SLAB, 3 * SLAB)


def groups(*sizes):
    return [range(sum(sizes[:i]), sum(sizes[: i + 1])) for i in range(len(sizes))]


OWN_GROUPS = groups(4, 4, 4, 4, 4, 4)
GHOST_GROUPS = groups(8, 8, 8)
ORDER = [("own", 0), ("own", 1), ("own", 2), ("own", 3), ("own", 4), ("own", 5), ("ghost", 0), ("ghost", 1), ("ghost", 2)]
AHEAD = 2
STREAMED = 8
MESH = pl.DeviceIdType.MESH

dot = functools.partial(lax.dot_general, dimension_numbers=NT, preferred_element_type=jnp.float32)


def expand(x, row_agg):
    r2, r4, r6 = (pltpu.roll(x, s, 0) for s in (2, 4, 6))
    i = lax.broadcasted_iota(jnp.int32, (8, BS), 0)
    v = (jnp.where(i < 6, x, r6), jnp.where(i < 4, r6, r4), jnp.where(i < 2, r4, r2))
    agg = jnp.broadcast_to(x[6:7, :], (8, BS))
    rows = [jnp.where(row_agg[8 * k : 8 * k + 8] == agg, v[k % 3], 0.0) for k in range(6)]
    return jnp.concatenate(rows, axis=0).astype(jnp.bfloat16)


def split(x):
    high = x.astype(jnp.bfloat16)
    low = (x - high.astype(jnp.float32)).astype(jnp.bfloat16)
    return high, low


def kernel(
    count,
    a_hbm, t_hbm, slots_hbm, send_hbm, agg_hbm,
    out_ref,
    a_v, t_v, t8, te_own, te_gh, send_t, recv_t, g_hi, g_lo, l_hi, l_lo, l_gh, weight, acc, send_c, recv_c, result,
    slots, send_list, agg,
    a_sem, small_sem, st_sem, rt_sem, sc_sem, rc_sem,
):
    me = lax.axis_index("dom")
    small = [
        pltpu.make_async_copy(src, dst, small_sem.at[i])
        for i, (src, dst) in enumerate(
            ((agg_hbm, agg), (t_hbm, t_v), (send_hbm, send_list), (slots_hbm, slots))
        )
    ]
    for copy in small:
        copy.start()

    def own_copy(step):
        group = OWN_GROUPS[step]
        part = (pl.ds(group.start, len(group)), pl.ds(0, KO))
        return pltpu.make_async_copy(a_hbm.at[part], a_v.at[part], a_sem.at[0, step])

    def ghost_copy(step):
        group = GHOST_GROUPS[step]
        part = (pl.ds(group.start, len(group)), pl.ds(KO, KG))
        return pltpu.make_async_copy(a_hbm.at[part], a_v.at[part], a_sem.at[1, step])


    exists = [jnp.logical_and(me - o >= 0, me - o < count) for o in OFFSETS]
    recv_c[...] = jnp.zeros_like(recv_c)
    barrier = pltpu.get_barrier_semaphore()
    for p, o in enumerate(OFFSETS):
        @pl.when(exists[p])
        def _():
            pl.semaphore_signal(barrier, inc=1, device_id=(me - o,), device_id_type=MESH)

    for kind, step in ORDER[:AHEAD]:
        (own_copy if kind == "own" else ghost_copy)(step).start()
    for copy in small:
        copy.wait()
    for kind, step in ORDER[AHEAD:]:
        (own_copy if kind == "own" else ghost_copy)(step).start()

    iota = lax.broadcasted_iota(jnp.int32, (SLAB, BS), 0)
    row_agg = lax.shift_right_logical(iota * 43, 8).astype(jnp.float32)

    for m in range(MODES):
        t8[:, m, :] = t_v[m].astype(jnp.float32)
    for b in range(RB):
        own_agg = (agg[b, 0] - me * 8).astype(jnp.float32)
        t8[b, MODES:8, :] = jnp.full((2, BS), own_agg, jnp.float32)
    for p in range(4):
        for g in range(0, GH, 2):
            pair = [t8[send_list[0, p, g + h]] for h in range(2)]
            send_t[p, g * 8 : g * 8 + 16, :] = jnp.concatenate(pair, axis=0).astype(jnp.bfloat16)

    def own_table(b, c):
        te_own[b] = expand(t8[b], row_agg)
        return c

    lax.fori_loop(0, RB, own_table, 0, unroll=4)

    total = sum(e.astype(jnp.int32) for e in exists)
    pl.semaphore_wait(barrier, total)

    def t_copy(p):
        return pltpu.make_async_remote_copy(
            src_ref=send_t.at[p], dst_ref=recv_t.at[p], send_sem=st_sem.at[p], recv_sem=rt_sem.at[p],
            device_id=(me + OFFSETS[p],), device_id_type=MESH,
        )

    for p in range(4):
        @pl.when(exists[3 - p])
        def _():
            t_copy(p).start()

    def zero_table(v, c):
        te_gh[v] = jnp.zeros((4 * SLAB, BS), jnp.bfloat16)
        return c

    lax.fori_loop(0, 4 * GH, zero_table, 0, unroll=4)

    eye = lax.broadcasted_iota(jnp.int32, (BS, BS), 0) == lax.broadcasted_iota(jnp.int32, (BS, BS), 1)

    def own_rows(step):
        own_copy(step).wait()
        for b in OWN_GROUPS[step]:
            still, moving = range(KO - STREAMED), range(KO - STREAMED, KO)
            table, tiles = (
                [jnp.concatenate([f(s) for s in part], axis=1) for part in (still, moving)]
                for f in (lambda s: te_own[slots[b, s]], lambda s: a_v[b, s])
            )
            grouped = dot(table[0], tiles[0]) + dot(tiles[1], table[1]).T
            diagonal = jnp.sum(
                jnp.where(eye, a_v[b, 0].astype(jnp.float32), 0.0), axis=0, keepdims=True
            )
            w = -OMEGA * (1.0 / diagonal)
            weight[b] = jnp.broadcast_to(w, (8, BS))
            g_hi[b, OWN, :], g_lo[b, OWN, :] = split(grouped)
            l_hi[b], l_lo[b] = split(te_own[b].astype(jnp.float32) + grouped * w)

    def ghost_tables():
        for p in range(4):
            @pl.when(exists[p])
            def _():
                t_copy(p).wait_recv()

        for p in range(4):
            def ghost_table(g, c):
                x = recv_t[p, pl.ds(pl.multiple_of(g * 16, 16), 16), :].astype(jnp.float32)
                rows = slice((3 - p) * SLAB, (4 - p) * SLAB)
                te_gh[p * GH + 2 * g, rows, :] = expand(x[0:8], row_agg)
                te_gh[p * GH + 2 * g + 1, rows, :] = expand(x[8:16], row_agg)
                return c

            lax.fori_loop(0, GH // 2, ghost_table, 0, unroll=2)

    def ghost_rows(step):
        ghost_copy(step).wait()
        for b in GHOST_GROUPS[step]:
            lhs = jnp.concatenate(
                [te_gh[jnp.maximum(slots[b, s] - RB, 0)] for s in range(KO, K)], axis=1
            )
            rhs = jnp.concatenate([a_v[b, s] for s in range(KO, K)], axis=1)
            ghost = dot(lhs, rhs)
            l_gh[b] = (ghost * weight[b, 0:1]).astype(jnp.bfloat16)
            high, low = split(ghost)
            for part, whole in ((g_hi, high), (g_lo, low)):
                part[b, : 2 * SLAB, :] = whole[: 2 * SLAB]
                part[b, 3 * SLAB :, :] = whole[2 * SLAB :]

    def joined(ref, group):
        return jnp.concatenate([ref[b] for b in group], axis=1)

    def contract(step):
        group = GHOST_GROUPS[step]
        return dot(joined(l_gh, group), joined(g_hi, group))

    for kind, step in ORDER:
        if kind == "own":
            own_rows(step)
            continue
        if step == 0:
            ghost_tables()
        ghost_rows(step)
        if step == 1:
            acc[...] = contract(0)
        elif step > 1:
            acc[...] += contract(step - 1)
    last = acc[...] + contract(len(GHOST_GROUPS) - 1)

    def c_copy(p):
        return pltpu.make_async_remote_copy(
            src_ref=send_c.at[p], dst_ref=recv_c.at[p], send_sem=sc_sem.at[p], recv_sem=rc_sem.at[p],
            device_id=(me - OFFSETS[p],), device_id_type=MESH,
        )

    for p in range(4):
        rows = slice((3 - p) * SLAB, (4 - p) * SLAB)
        send_c[p, :, 0:SPAN] = last[rows].astype(jnp.bfloat16)
        send_c[p, :, SPAN:256] = jnp.zeros((SLAB, 256 - SPAN), jnp.bfloat16)
    for p in (0, 3, 1, 2):
        @pl.when(exists[p])
        def _():
            c_copy(p).start()

    every = range(RB)
    both = dot(jnp.concatenate([joined(l_hi, every), joined(l_lo, every)], axis=0), joined(g_hi, every))
    mine = both[:SLAB] + both[SLAB:] + dot(joined(l_hi, every), joined(g_lo, every))

    zeros = jnp.zeros((SLAB, 256), jnp.float32)

    def placed(x, by):
        wide = jnp.concatenate([x, zeros], axis=1)
        return wide if by == 0 else pltpu.roll(wide, by, 1)

    summed = jnp.concatenate([mine, zeros[:, : 256 - SPAN]], axis=1)
    summed = placed(summed, 2 * SLAB)
    for p, o in enumerate(OFFSETS):
        @pl.when(exists[3 - p])
        def _():
            c_copy(p).wait_recv()
    for p, o in enumerate(OFFSETS):
        summed = summed + placed(recv_c[p].astype(jnp.float32), (o + 2) * SLAB)
    for t in range(4):
        result[t] = summed[:, t * BS : (t + 1) * BS]
    for m in range(MODES):
        for t in range(4):
            size = min(BS, 9 * SLAB - t * BS)
            rows = result[t, pl.ds(m, 8, stride=MODES), :]
            out_ref[m, :, t * BS : t * BS + size] = rows[:, :size]
    for p in range(4):
        @pl.when(exists[3 - p])
        def _():
            t_copy(p).wait_send()

        @pl.when(exists[p])
        def _():
            c_copy(p).wait_send()


def solution(mesh):
    count = mesh.shape["dom"]
    call = pl.pallas_call(
        functools.partial(kernel, count),
        out_shape=pltpu.VMEM((MODES, 8, 9 * SLAB), jnp.float32),
        in_specs=[pl.BlockSpec(memory_space=pl.ANY)] * 5,
        out_specs=pl.BlockSpec(memory_space=pltpu.VMEM),
        scratch_shapes=[
            pltpu.VMEM((RB, K, BS, BS), jnp.bfloat16),
            pltpu.VMEM((MODES, RB, BS), jnp.bfloat16),
            pltpu.VMEM((RB, 8, BS), jnp.float32),
            pltpu.VMEM((RB, SLAB, BS), jnp.bfloat16),
            pltpu.VMEM((4 * GH, 4 * SLAB, BS), jnp.bfloat16),
            pltpu.VMEM((4, GH * 8, BS), jnp.bfloat16),
            pltpu.VMEM((4, GH * 8, BS), jnp.bfloat16),
            pltpu.VMEM((RB, SPAN, BS), jnp.bfloat16),
            pltpu.VMEM((RB, SPAN, BS), jnp.bfloat16),
            pltpu.VMEM((RB, SLAB, BS), jnp.bfloat16),
            pltpu.VMEM((RB, SLAB, BS), jnp.bfloat16),
            pltpu.VMEM((RB, 4 * SLAB, BS), jnp.bfloat16),
            pltpu.VMEM((RB, 8, BS), jnp.float32),
            pltpu.VMEM((4 * SLAB, SPAN), jnp.float32),
            pltpu.VMEM((4, SLAB, 256), jnp.bfloat16),
            pltpu.VMEM((4, SLAB, 256), jnp.bfloat16),
            pltpu.VMEM((4, SLAB, BS), jnp.float32),
            pltpu.SMEM((RB, K), jnp.int32),
            pltpu.SMEM((1, 4, GH), jnp.int32),
            pltpu.SMEM((RB, K), jnp.int32),
            pltpu.SemaphoreType.DMA((2, RB)),
            pltpu.SemaphoreType.DMA((4,)),
            pltpu.SemaphoreType.DMA((4,)),
            pltpu.SemaphoreType.DMA((4,)),
            pltpu.SemaphoreType.DMA((4,)),
            pltpu.SemaphoreType.DMA((4,)),
        ],
        compiler_params=pltpu.CompilerParams(
            collective_id=0, has_side_effects=True, vmem_limit_bytes=56 << 20
        ),
    )

    def body(matrix_tiles, tentative, column_slots, send_list, column_aggregate):
        by_mode = call(
            matrix_tiles, tentative.transpose(1, 0, 2), column_slots, send_list, column_aggregate
        )
        return by_mode.transpose(1, 0, 2)

    placed = (
        P("dom", None, None, None),
        P("dom", None, None),
        P("dom", None),
        P("dom", None, None),
        P("dom", None),
    )
    return jax.shard_map(
        body, mesh=mesh, in_specs=placed, out_specs=P("dom", None, None), check_vma=False
    )
```

```python
import functools

import jax
import jax.numpy as jnp
from jax import lax
from jax.experimental import pallas as pl
from jax.experimental.pallas import tpu as pltpu
from jax.sharding import PartitionSpec as P

OMEGA = 0.6
RB = 24
K = 27
KO = 18
KG = 9
BS = 128
MODES = 6
GH = 16
SLAB = 48
SPAN = 5 * SLAB
OFFSETS = (-2, -1, 1, 2)
NT = (((1,), (1,)), ((), ()))
OWN = slice(2 * SLAB, 3 * SLAB)


def groups(*sizes):
    return [range(sum(sizes[:i]), sum(sizes[: i + 1])) for i in range(len(sizes))]


OWN_GROUPS = groups(4, 4, 4, 4, 4, 4)
GHOST_GROUPS = groups(8, 8, 8)
ORDER = [("own", 0), ("own", 1), ("own", 2), ("own", 3), ("own", 4), ("own", 5), ("ghost", 0), ("ghost", 1), ("ghost", 2)]
AHEAD = 2
GHOST_STREAMED = 4
PARTS = 3
GREET = 1
STREAMED = 8
MESH = pl.DeviceIdType.MESH

dot = functools.partial(lax.dot_general, dimension_numbers=NT, preferred_element_type=jnp.float32)


def expand(x, row_agg):
    r2, r4, r6 = (pltpu.roll(x, s, 0) for s in (2, 4, 6))
    i = lax.broadcasted_iota(jnp.int32, (8, BS), 0)
    v = (jnp.where(i < 6, x, r6), jnp.where(i < 4, r6, r4), jnp.where(i < 2, r4, r2))
    agg = jnp.broadcast_to(x[6:7, :], (8, BS))
    rows = [jnp.where(row_agg[8 * k : 8 * k + 8] == agg, v[k % 3], 0.0) for k in range(6)]
    return jnp.concatenate(rows, axis=0).astype(jnp.bfloat16)


def split(x):
    high = x.astype(jnp.bfloat16)
    low = (x - high.astype(jnp.float32)).astype(jnp.bfloat16)
    return high, low


def kernel(
    count,
    a_hbm, t_hbm, slots_hbm, send_hbm, agg_hbm,
    out_ref,
    a_v, t_v, t8, te_own, te_gh, send_t, recv_t, g_hi, g_lo, l_hi, l_lo, l_gh, weight, acc, send_c, recv_c, result,
    slots, send_list, agg,
    a_sem, small_sem, st_sem, rt_sem, sc_sem, rc_sem,
):
    me = lax.axis_index("dom")
    small = [
        pltpu.make_async_copy(src, dst, small_sem.at[i])
        for i, (src, dst) in enumerate(
            ((agg_hbm, agg), (t_hbm, t_v), (send_hbm, send_list), (slots_hbm, slots))
        )
    ]
    for copy in small:
        copy.start()

    def own_copy(step):
        group = OWN_GROUPS[step]
        part = (pl.ds(group.start, len(group)), pl.ds(0, KO))
        return pltpu.make_async_copy(a_hbm.at[part], a_v.at[part], a_sem.at[0, step])

    def ghost_copy(step):
        group = GHOST_GROUPS[step]
        part = (pl.ds(group.start, len(group)), pl.ds(KO, KG))
        return pltpu.make_async_copy(a_hbm.at[part], a_v.at[part], a_sem.at[1, step])


    exists = [jnp.logical_and(me - o >= 0, me - o < count) for o in OFFSETS]
    recv_c[...] = jnp.zeros_like(recv_c)
    barrier = pltpu.get_barrier_semaphore()
    for p, o in enumerate(OFFSETS):
        @pl.when(exists[p])
        def _():
            pl.semaphore_signal(barrier, inc=1, device_id=(me - o,), device_id_type=MESH)

    for kind, step in ORDER[:AHEAD]:
        (own_copy if kind == "own" else ghost_copy)(step).start()
    for copy in small:
        copy.wait()
    for kind, step in ORDER[AHEAD:]:
        (own_copy if kind == "own" else ghost_copy)(step).start()

    iota = lax.broadcasted_iota(jnp.int32, (SLAB, BS), 0)
    row_agg = lax.shift_right_logical(iota * 43, 8).astype(jnp.float32)

    for m in range(MODES):
        t8[:, m, :] = t_v[m].astype(jnp.float32)
    for b in range(RB):
        own_agg = (agg[b, 0] - me * 8).astype(jnp.float32)
        t8[b, MODES:8, :] = jnp.full((2, BS), own_agg, jnp.float32)
    for p in range(4):
        for g in range(0, GH, 2):
            pair = [t8[send_list[0, p, g + h]] for h in range(2)]
            send_t[p, g * 8 : g * 8 + 16, :] = jnp.concatenate(pair, axis=0).astype(jnp.bfloat16)

    def own_table(b, c):
        te_own[b] = expand(t8[b], row_agg)
        return c

    lax.fori_loop(0, RB, own_table, 0, unroll=4)

    def t_copy(p):
        return pltpu.make_async_remote_copy(
            src_ref=send_t.at[p], dst_ref=recv_t.at[p], send_sem=st_sem.at[p], recv_sem=rt_sem.at[p],
            device_id=(me + OFFSETS[p],), device_id_type=MESH,
        )

    def send_blocks():
        total = sum(e.astype(jnp.int32) for e in exists)
        pl.semaphore_wait(barrier, total)

        for p in range(4):
            @pl.when(exists[3 - p])
            def _():
                t_copy(p).start()

    def zero_table(v, c):
        te_gh[v] = jnp.zeros((4 * SLAB, BS), jnp.bfloat16)
        return c

    lax.fori_loop(0, 4 * GH, zero_table, 0, unroll=4)

    eye = lax.broadcasted_iota(jnp.int32, (BS, BS), 0) == lax.broadcasted_iota(jnp.int32, (BS, BS), 1)

    def own_rows(step):
        own_copy(step).wait()
        for b in OWN_GROUPS[step]:
            still, moving = range(KO - STREAMED), range(KO - STREAMED, KO)
            table, tiles = (
                [jnp.concatenate([f(s) for s in part], axis=1) for part in (still, moving)]
                for f in (lambda s: te_own[slots[b, s]], lambda s: a_v[b, s])
            )
            grouped = dot(table[0], tiles[0]) + dot(tiles[1], table[1]).T
            diagonal = jnp.sum(
                jnp.where(eye, a_v[b, 0].astype(jnp.float32), 0.0), axis=0, keepdims=True
            )
            w = -OMEGA * (1.0 / diagonal)
            weight[b] = jnp.broadcast_to(w, (8, BS))
            g_hi[b, OWN, :], g_lo[b, OWN, :] = split(grouped)
            l_hi[b], l_lo[b] = split(te_own[b].astype(jnp.float32) + grouped * w)

    def ghost_tables(p):
        @pl.when(exists[p])
        def _():
            t_copy(p).wait_recv()

        def ghost_table(g, c):
            x = recv_t[p, pl.ds(pl.multiple_of(g * 16, 16), 16), :].astype(jnp.float32)
            rows = slice((3 - p) * SLAB, (4 - p) * SLAB)
            te_gh[p * GH + 2 * g, rows, :] = expand(x[0:8], row_agg)
            te_gh[p * GH + 2 * g + 1, rows, :] = expand(x[8:16], row_agg)
            return c

        lax.fori_loop(0, GH // 2, ghost_table, 0, unroll=8)

    def ghost_rows(step):
        if step % PARTS == 0:
            for later in range(step, min(step + PARTS, len(GHOST_GROUPS))):
                ghost_copy(later).wait()
        for b in GHOST_GROUPS[step]:
            table = [te_gh[jnp.maximum(slots[b, s] - RB, 0)] for s in range(KO, K)]
            tile = [a_v[b, s] for s in range(KO, K)]
            cut = KG - GHOST_STREAMED
            ghost = dot(jnp.concatenate(table[:cut], axis=1), jnp.concatenate(tile[:cut], axis=1))
            if GHOST_STREAMED:
                ghost = ghost + dot(jnp.concatenate(tile[cut:], axis=1), jnp.concatenate(table[cut:], axis=1)).T
            l_gh[b] = (ghost * weight[b, 0:1]).astype(jnp.bfloat16)
            high, low = split(ghost)
            for part, whole in ((g_hi, high), (g_lo, low)):
                part[b, : 2 * SLAB, :] = whole[: 2 * SLAB]
                part[b, 3 * SLAB :, :] = whole[2 * SLAB :]

    def joined(ref, group):
        return jnp.concatenate([ref[b] for b in group], axis=1)

    def contract(step):
        group = GHOST_GROUPS[step]
        return dot(joined(l_gh, group), joined(g_hi, group))

    for kind, step in ORDER:
        if kind == "own":
            if step == GREET:
                send_blocks()
            own_rows(step)
            continue
        if step == 0:
            for p in (2, 3, 1, 0):
                ghost_tables(p)
        ghost_rows(step)
        if step == 1:
            acc[...] = contract(0)
        elif step > 1:
            acc[...] += contract(step - 1)
    last = acc[...] + contract(len(GHOST_GROUPS) - 1)

    def c_copy(p):
        return pltpu.make_async_remote_copy(
            src_ref=send_c.at[p], dst_ref=recv_c.at[p], send_sem=sc_sem.at[p], recv_sem=rc_sem.at[p],
            device_id=(me - OFFSETS[p],), device_id_type=MESH,
        )

    for p in range(4):
        rows = slice((3 - p) * SLAB, (4 - p) * SLAB)
        send_c[p, :, 0:SPAN] = last[rows].astype(jnp.bfloat16)
        send_c[p, :, SPAN:256] = jnp.zeros((SLAB, 256 - SPAN), jnp.bfloat16)
    for p in (0, 1, 3, 2):
        @pl.when(exists[p])
        def _():
            c_copy(p).start()

    every = range(RB)
    both = dot(jnp.concatenate([joined(l_hi, every), joined(l_lo, every)], axis=0), joined(g_hi, every))
    mine = both[:SLAB] + both[SLAB:] + dot(joined(l_hi, every), joined(g_lo, every))

    zeros = jnp.zeros((SLAB, 256), jnp.float32)

    def placed(x, by):
        wide = jnp.concatenate([x, zeros], axis=1)
        return wide if by == 0 else pltpu.roll(wide, by, 1)

    summed = jnp.concatenate([mine, zeros[:, : 256 - SPAN]], axis=1)
    summed = placed(summed, 2 * SLAB)
    for p in (2, 3, 1, 0):
        @pl.when(exists[3 - p])
        def _():
            c_copy(p).wait_recv()

        summed = summed + placed(recv_c[p].astype(jnp.float32), (OFFSETS[p] + 2) * SLAB)
    for t in range(4):
        result[t] = summed[:, t * BS : (t + 1) * BS]
    for m in range(MODES):
        for t in range(4):
            size = min(BS, 9 * SLAB - t * BS)
            rows = result[t, pl.ds(m, 8, stride=MODES), :]
            out_ref[m, :, t * BS : t * BS + size] = rows[:, :size]
    for p in range(4):
        @pl.when(exists[3 - p])
        def _():
            t_copy(p).wait_send()

        @pl.when(exists[p])
        def _():
            c_copy(p).wait_send()


def solution(mesh):
    count = mesh.shape["dom"]
    call = pl.pallas_call(
        functools.partial(kernel, count),
        out_shape=pltpu.VMEM((MODES, 8, 9 * SLAB), jnp.float32),
        in_specs=[pl.BlockSpec(memory_space=pl.ANY)] * 5,
        out_specs=pl.BlockSpec(memory_space=pltpu.VMEM),
        scratch_shapes=[
            pltpu.VMEM((RB, K, BS, BS), jnp.bfloat16),
            pltpu.VMEM((MODES, RB, BS), jnp.bfloat16),
            pltpu.VMEM((RB, 8, BS), jnp.float32),
            pltpu.VMEM((RB, SLAB, BS), jnp.bfloat16),
            pltpu.VMEM((4 * GH, 4 * SLAB, BS), jnp.bfloat16),
            pltpu.VMEM((4, GH * 8, BS), jnp.bfloat16),
            pltpu.VMEM((4, GH * 8, BS), jnp.bfloat16),
            pltpu.VMEM((RB, SPAN, BS), jnp.bfloat16),
            pltpu.VMEM((RB, SPAN, BS), jnp.bfloat16),
            pltpu.VMEM((RB, SLAB, BS), jnp.bfloat16),
            pltpu.VMEM((RB, SLAB, BS), jnp.bfloat16),
            pltpu.VMEM((RB, 4 * SLAB, BS), jnp.bfloat16),
            pltpu.VMEM((RB, 8, BS), jnp.float32),
            pltpu.VMEM((4 * SLAB, SPAN), jnp.float32),
            pltpu.VMEM((4, SLAB, 256), jnp.bfloat16),
            pltpu.VMEM((4, SLAB, 256), jnp.bfloat16),
            pltpu.VMEM((4, SLAB, BS), jnp.float32),
            pltpu.SMEM((RB, K), jnp.int32),
            pltpu.SMEM((1, 4, GH), jnp.int32),
            pltpu.SMEM((RB, K), jnp.int32),
            pltpu.SemaphoreType.DMA((2, RB)),
            pltpu.SemaphoreType.DMA((4,)),
            pltpu.SemaphoreType.DMA((4,)),
            pltpu.SemaphoreType.DMA((4,)),
            pltpu.SemaphoreType.DMA((4,)),
            pltpu.SemaphoreType.DMA((4,)),
        ],
        compiler_params=pltpu.CompilerParams(
            collective_id=0, has_side_effects=True, vmem_limit_bytes=56 << 20
        ),
    )

    def body(matrix_tiles, tentative, column_slots, send_list, column_aggregate):
        by_mode = call(
            matrix_tiles, tentative.transpose(1, 0, 2), column_slots, send_list, column_aggregate
        )
        return by_mode.transpose(1, 0, 2)

    placed = (
        P("dom", None, None, None),
        P("dom", None, None),
        P("dom", None),
        P("dom", None, None),
        P("dom", None),
    )
    return jax.shard_map(
        body, mesh=mesh, in_specs=placed, out_specs=P("dom", None, None), check_vma=False
    )
```

```python
import functools

import jax
import jax.numpy as jnp
from jax import lax
from jax.experimental import pallas as pl
from jax.experimental.pallas import tpu as pltpu
from jax.sharding import PartitionSpec as P

OMEGA = 0.6
RB = 24
K = 27
KO = 18
KG = 9
BS = 128
MODES = 6
GH = 16
SLAB = 48
SPAN = 5 * SLAB
OFFSETS = (-2, -1, 1, 2)
NT = (((1,), (1,)), ((), ()))
OWN = slice(2 * SLAB, 3 * SLAB)


def groups(*sizes):
    return [range(sum(sizes[:i]), sum(sizes[: i + 1])) for i in range(len(sizes))]


OWN_GROUPS = groups(4, 4, 4, 4, 4, 4)
GHOST_GROUPS = groups(8, 8, 8)
ORDER = [("own", 0), ("own", 1), ("own", 2), ("own", 3), ("own", 4), ("own", 5), ("ghost", 0), ("ghost", 1), ("ghost", 2)]
AHEAD = 2
GHOST_STREAMED = 4
PARTS = 3
GREET = 1
STREAMED = 8
MESH = pl.DeviceIdType.MESH

dot = functools.partial(lax.dot_general, dimension_numbers=NT, preferred_element_type=jnp.float32)


def expand(x, row_agg):
    r2, r4, r6 = (pltpu.roll(x, s, 0) for s in (2, 4, 6))
    i = lax.broadcasted_iota(jnp.int32, (8, BS), 0)
    v = (jnp.where(i < 6, x, r6), jnp.where(i < 4, r6, r4), jnp.where(i < 2, r4, r2))
    agg = jnp.broadcast_to(x[6:7, :], (8, BS))
    rows = [jnp.where(row_agg[8 * k : 8 * k + 8] == agg, v[k % 3], 0.0) for k in range(6)]
    return jnp.concatenate(rows, axis=0).astype(jnp.bfloat16)


def split(x):
    high = x.astype(jnp.bfloat16)
    low = (x - high.astype(jnp.float32)).astype(jnp.bfloat16)
    return high, low


def kernel(
    count,
    a_hbm, t_hbm, slots_hbm, send_hbm, agg_hbm,
    out_ref,
    a_v, t_v, t8, te_own, te_gh, send_t, recv_t, g_hi, g_lo, l_hi, l_lo, l_gh, weight, acc, send_c, recv_c, result,
    slots, send_list, agg,
    a_sem, small_sem, st_sem, rt_sem, sc_sem, rc_sem,
):
    me = lax.axis_index("dom")
    exists = [jnp.logical_and(me - o >= 0, me - o < count) for o in OFFSETS]
    recv_c[...] = jnp.zeros_like(recv_c)
    send_c[:, :, SPAN:256] = jnp.zeros((4, SLAB, 256 - SPAN), jnp.bfloat16)
    barrier = pltpu.get_barrier_semaphore()
    for p, o in enumerate(OFFSETS):
        @pl.when(exists[p])
        def _():
            pl.semaphore_signal(barrier, inc=1, device_id=(me - o,), device_id_type=MESH)

    small = [
        pltpu.make_async_copy(src, dst, small_sem.at[i])
        for i, (src, dst) in enumerate(
            ((agg_hbm, agg), (t_hbm, t_v), (send_hbm, send_list), (slots_hbm, slots))
        )
    ]
    for copy in small:
        copy.start()

    def own_copy(step):
        group = OWN_GROUPS[step]
        part = (pl.ds(group.start, len(group)), pl.ds(0, KO))
        return pltpu.make_async_copy(a_hbm.at[part], a_v.at[part], a_sem.at[0, step])

    def ghost_copy(step):
        group = GHOST_GROUPS[step]
        part = (pl.ds(group.start, len(group)), pl.ds(KO, KG))
        return pltpu.make_async_copy(a_hbm.at[part], a_v.at[part], a_sem.at[1, step])


    for kind, step in ORDER[:AHEAD]:
        (own_copy if kind == "own" else ghost_copy)(step).start()
    for copy in small:
        copy.wait()
    for kind, step in ORDER[AHEAD:]:
        (own_copy if kind == "own" else ghost_copy)(step).start()

    iota = lax.broadcasted_iota(jnp.int32, (SLAB, BS), 0)
    row_agg = lax.shift_right_logical(iota * 43, 8).astype(jnp.float32)

    for m in range(MODES):
        t8[:, m, :] = t_v[m].astype(jnp.float32)
    for b in range(RB):
        own_agg = (agg[b, 0] - me * 8).astype(jnp.float32)
        t8[b, MODES:8, :] = jnp.full((2, BS), own_agg, jnp.float32)
    for p in range(4):
        for g in range(0, GH, 2):
            pair = [t8[send_list[0, p, g + h]] for h in range(2)]
            send_t[p, g * 8 : g * 8 + 16, :] = jnp.concatenate(pair, axis=0).astype(jnp.bfloat16)

    def own_table(b, c):
        te_own[b] = expand(t8[b], row_agg)
        return c

    lax.fori_loop(0, RB, own_table, 0, unroll=4)

    def t_copy(p):
        return pltpu.make_async_remote_copy(
            src_ref=send_t.at[p], dst_ref=recv_t.at[p], send_sem=st_sem.at[p], recv_sem=rt_sem.at[p],
            device_id=(me + OFFSETS[p],), device_id_type=MESH,
        )

    def send_blocks():
        total = sum(e.astype(jnp.int32) for e in exists)
        pl.semaphore_wait(barrier, total)

        for p in range(4):
            @pl.when(exists[3 - p])
            def _():
                t_copy(p).start()

    def zero_table(v, c):
        te_gh[v] = jnp.zeros((4 * SLAB, BS), jnp.bfloat16)
        return c

    lax.fori_loop(0, 4 * GH, zero_table, 0, unroll=4)

    eye = lax.broadcasted_iota(jnp.int32, (BS, BS), 0) == lax.broadcasted_iota(jnp.int32, (BS, BS), 1)

    def own_rows(step):
        own_copy(step).wait()
        for b in OWN_GROUPS[step]:
            still, moving = range(KO - STREAMED), range(KO - STREAMED, KO)
            table, tiles = (
                [jnp.concatenate([f(s) for s in part], axis=1) for part in (still, moving)]
                for f in (lambda s: te_own[slots[b, s]], lambda s: a_v[b, s])
            )
            grouped = dot(table[0], tiles[0]) + dot(tiles[1], table[1]).T
            diagonal = jnp.sum(
                jnp.where(eye, a_v[b, 0].astype(jnp.float32), 0.0), axis=0, keepdims=True
            )
            w = -OMEGA * (1.0 / diagonal)
            weight[b] = jnp.broadcast_to(w, (8, BS))
            g_hi[b, OWN, :], g_lo[b, OWN, :] = split(grouped)
            l_hi[b], l_lo[b] = split(te_own[b].astype(jnp.float32) + grouped * w)

    def ghost_tables(p):
        @pl.when(exists[p])
        def _():
            t_copy(p).wait_recv()

        def ghost_table(g, c):
            x = recv_t[p, pl.ds(pl.multiple_of(g * 16, 16), 16), :].astype(jnp.float32)
            rows = slice((3 - p) * SLAB, (4 - p) * SLAB)
            te_gh[p * GH + 2 * g, rows, :] = expand(x[0:8], row_agg)
            te_gh[p * GH + 2 * g + 1, rows, :] = expand(x[8:16], row_agg)
            return c

        lax.fori_loop(0, GH // 2, ghost_table, 0, unroll=8)

    def ghost_rows(step):
        if step % PARTS == 0:
            for later in range(step, min(step + PARTS, len(GHOST_GROUPS))):
                ghost_copy(later).wait()
        for b in GHOST_GROUPS[step]:
            table = [te_gh[jnp.maximum(slots[b, s] - RB, 0)] for s in range(KO, K)]
            tile = [a_v[b, s] for s in range(KO, K)]
            cut = KG - GHOST_STREAMED
            ghost = dot(jnp.concatenate(table[:cut], axis=1), jnp.concatenate(tile[:cut], axis=1))
            if GHOST_STREAMED:
                ghost = ghost + dot(jnp.concatenate(tile[cut:], axis=1), jnp.concatenate(table[cut:], axis=1)).T
            l_gh[b] = (ghost * weight[b, 0:1]).astype(jnp.bfloat16)
            high, low = split(ghost)
            for part, whole in ((g_hi, high), (g_lo, low)):
                part[b, : 2 * SLAB, :] = whole[: 2 * SLAB]
                part[b, 3 * SLAB :, :] = whole[2 * SLAB :]

    def joined(ref, group):
        return jnp.concatenate([ref[b] for b in group], axis=1)

    def contract(step):
        group = GHOST_GROUPS[step]
        return dot(joined(l_gh, group), joined(g_hi, group))

    for kind, step in ORDER:
        if kind == "own":
            if step == GREET:
                send_blocks()
            own_rows(step)
            continue
        if step == 0:
            for p in (2, 3, 1, 0):
                ghost_tables(p)
        ghost_rows(step)
        if step == 1:
            acc[...] = contract(0)
        elif step > 1:
            acc[...] += contract(step - 1)
    last = acc[...] + contract(len(GHOST_GROUPS) - 1)

    def c_copy(p):
        return pltpu.make_async_remote_copy(
            src_ref=send_c.at[p], dst_ref=recv_c.at[p], send_sem=sc_sem.at[p], recv_sem=rc_sem.at[p],
            device_id=(me - OFFSETS[p],), device_id_type=MESH,
        )

    for p in (0, 1, 3, 2):
        rows = slice((3 - p) * SLAB, (4 - p) * SLAB)
        send_c[p, :, 0:SPAN] = last[rows].astype(jnp.bfloat16)
    for p in (0, 1, 3, 2):
        @pl.when(exists[p])
        def _():
            c_copy(p).start()

    every = range(RB)
    both = dot(jnp.concatenate([joined(l_hi, every), joined(l_lo, every)], axis=0), joined(g_hi, every))
    mine = both[:SLAB] + both[SLAB:] + dot(joined(l_hi, every), joined(g_lo, every))

    zeros = jnp.zeros((SLAB, 256), jnp.float32)

    def placed(x, by):
        wide = jnp.concatenate([x, zeros], axis=1)
        return wide if by == 0 else pltpu.roll(wide, by, 1)

    summed = jnp.concatenate([mine, zeros[:, : 256 - SPAN]], axis=1)
    summed = placed(summed, 2 * SLAB)
    for p in (2, 3, 1, 0):
        @pl.when(exists[3 - p])
        def _():
            c_copy(p).wait_recv()

        summed = summed + placed(recv_c[p].astype(jnp.float32), (OFFSETS[p] + 2) * SLAB)
    for t in range(4):
        result[t] = summed[:, t * BS : (t + 1) * BS]
    for m in range(MODES):
        for t in range(4):
            size = min(BS, 9 * SLAB - t * BS)
            rows = result[t, pl.ds(m, 8, stride=MODES), :]
            out_ref[m, :, t * BS : t * BS + size] = rows[:, :size]
    for p in range(4):
        @pl.when(exists[3 - p])
        def _():
            t_copy(p).wait_send()

        @pl.when(exists[p])
        def _():
            c_copy(p).wait_send()


def solution(mesh):
    count = mesh.shape["dom"]
    call = pl.pallas_call(
        functools.partial(kernel, count),
        out_shape=pltpu.VMEM((MODES, 8, 9 * SLAB), jnp.float32),
        in_specs=[pl.BlockSpec(memory_space=pl.ANY)] * 5,
        out_specs=pl.BlockSpec(memory_space=pltpu.VMEM),
        scratch_shapes=[
            pltpu.VMEM((RB, K, BS, BS), jnp.bfloat16),
            pltpu.VMEM((MODES, RB, BS), jnp.bfloat16),
            pltpu.VMEM((RB, 8, BS), jnp.float32),
            pltpu.VMEM((RB, SLAB, BS), jnp.bfloat16),
            pltpu.VMEM((4 * GH, 4 * SLAB, BS), jnp.bfloat16),
            pltpu.VMEM((4, GH * 8, BS), jnp.bfloat16),
            pltpu.VMEM((4, GH * 8, BS), jnp.bfloat16),
            pltpu.VMEM((RB, SPAN, BS), jnp.bfloat16),
            pltpu.VMEM((RB, SPAN, BS), jnp.bfloat16),
            pltpu.VMEM((RB, SLAB, BS), jnp.bfloat16),
            pltpu.VMEM((RB, SLAB, BS), jnp.bfloat16),
            pltpu.VMEM((RB, 4 * SLAB, BS), jnp.bfloat16),
            pltpu.VMEM((RB, 8, BS), jnp.float32),
            pltpu.VMEM((4 * SLAB, SPAN), jnp.float32),
            pltpu.VMEM((4, SLAB, 256), jnp.bfloat16),
            pltpu.VMEM((4, SLAB, 256), jnp.bfloat16),
            pltpu.VMEM((4, SLAB, BS), jnp.float32),
            pltpu.SMEM((RB, K), jnp.int32),
            pltpu.SMEM((1, 4, GH), jnp.int32),
            pltpu.SMEM((RB, K), jnp.int32),
            pltpu.SemaphoreType.DMA((2, RB)),
            pltpu.SemaphoreType.DMA((4,)),
            pltpu.SemaphoreType.DMA((4,)),
            pltpu.SemaphoreType.DMA((4,)),
            pltpu.SemaphoreType.DMA((4,)),
            pltpu.SemaphoreType.DMA((4,)),
        ],
        compiler_params=pltpu.CompilerParams(
            collective_id=0, has_side_effects=True, vmem_limit_bytes=56 << 20
        ),
    )

    def body(matrix_tiles, tentative, column_slots, send_list, column_aggregate):
        by_mode = call(
            matrix_tiles, tentative.transpose(1, 0, 2), column_slots, send_list, column_aggregate
        )
        return by_mode.transpose(1, 0, 2)

    placed = (
        P("dom", None, None, None),
        P("dom", None, None),
        P("dom", None),
        P("dom", None, None),
        P("dom", None),
    )
    return jax.shard_map(
        body, mesh=mesh, in_specs=placed, out_specs=P("dom", None, None), check_vma=False
    )
```
